32 devices in a mesh: sec: 4 (over y, x), ctx: 2 (over core), ch: 4 (over z).
Axes of the slice: x: 2, y: 2, z: 4, core: 2. Of those that a mesh axis runs over, the one named last changes fastest.
Arguments:
- inputs: bfloat16 [256, 4096], P('ctx', ('ch', 'sec')), may hold values from -2500 to 2500, as said below
- query_fields: bfloat16 [4, 256, 4096], P('sec', 'ctx', 'ch'), may hold values from -3 to 3
- key_fields: bfloat16 [4, 256, 4096], P('sec', 'ctx', 'ch'), may hold values from -4 to 4
- norm_gain: float32 [4096], P('ch'), may hold values from 0.1 to 1.9
- short_taps: float32 [2, 7, 4096], P(None, None, 'ch'), may hold values from -2 to 2
- medium_taps: float32 [128, 4096], P(None, 'ch'), may hold values from -0.5 to 0.5
- pole_rates: float32 [8, 4096], P(None, 'ch'), as said below
- pole_residues: float32 [8, 4096], P(None, 'ch'), may hold values from -2 to 2
- direct_term: float32 [4096], P('ch'), may hold values from -3 to 3
Outputs:
- mixed_stream: bfloat16 [256, 4096], P('ctx', ('ch', 'sec'))
The draws below stay inside these ranges and needn't reach their ends.
Inputs may be any that keep to these rules, and one draw needn't show every extreme that they name: `inputs`: scaled real values. `pole_rates`: Positive, from 0.2 / 256 to 1 / 30.
All inputs are finite; a program needn't handle non-finite values.
Results may differ from the reference program's by a relative error of at most 0.013.
Values may be sent and summed in bfloat16 or wider, within the bound.
A program may use at most 64 MiB of HBM per device.

```python
import math
import jax
import jax.numpy as jnp
from jax import lax

D = 4096
SHORT = 7
MEDIUM = 128
MODES = 8
SECS = 4
TOKENS = 256
N_SEC = 4
N_CH = 4


def draw_inputs(key, part):
    rows_key, rough_key, base_key = jax.random.split(key, 3)
    rises = jnp.arange(D, dtype=jnp.float32) / D
    base_values = jax.random.truncated_normal(base_key, -6.0, 6.0, (TOKENS, D), jnp.float32)
    row_scale = jnp.exp(jax.random.uniform(rows_key, (TOKENS, 1), jnp.float32, 0.0, math.log(10.0)))
    col_scale = jnp.exp(rises * math.log(10.0))
    roughness = jax.random.uniform(rough_key, (D,), jnp.float32, 0.5, 1.5)
    return (base_values * row_scale * (col_scale * roughness)[None]).astype(jnp.bfloat16)


def draw_pole_rates(key, part):
    pick_key, slow_key, fast_key = jax.random.split(key, 3)
    grid_shape = (MODES, D)
    slow_rates = jnp.exp(jax.random.uniform(slow_key, grid_shape, jnp.float32, math.log(0.2), math.log(2.0))) / TOKENS
    fast_rates = jnp.exp(jax.random.uniform(fast_key, grid_shape, jnp.float32, math.log(2.0 / TOKENS), math.log(1.0 / 30.0)))
    slow_share = 0.5
    picked = jax.random.uniform(pick_key, grid_shape, jnp.float32) < slow_share
    return jnp.where(picked, slow_rates, fast_rates).astype(jnp.float32)


def steps_of(own_key, shape, cuts, low, high):
    gain, own = 1.0, jax.random.fold_in(own_key, 6)
    for position, blocks in cuts:
        heights = jnp.exp(jax.random.uniform(jax.random.fold_in(own, position), (blocks,), jnp.float32, low / len(cuts), high / len(cuts)))
        gain = gain * jnp.repeat(heights, shape[position] // blocks).reshape([-1 if axis == position else 1 for axis in range(len(shape))])
    return gain


def centred(own_key, shape, width, bound, cuts=(), held_as=jnp.bfloat16):
    gain = steps_of(own_key, shape, cuts, -0.22, 0.18) if cuts else 1.0
    array = jax.random.normal(own_key, shape, jnp.float32) * width * gain
    return jnp.minimum(jnp.maximum(array, -bound), bound).astype(held_as)


def setup_inputs(seed: int = 0) -> dict:
    streams_of = jax.random.split(jax.random.key(seed), 10)
    return {
        "inputs": draw_inputs(jax.random.fold_in(streams_of[9], 71), 0),
        "query_fields": centred(streams_of[1], (SECS, TOKENS, D), 0.5, 3.0, ((0, 4), (1, 2), (2, 4))),
        "key_fields": centred(streams_of[2], (SECS, TOKENS, D), 1.0, 4.0, ((0, 4), (1, 2), (2, 4))),
        "norm_gain": jnp.clip(1.0 + 0.18 * jax.random.normal(streams_of[3], (D,), jnp.float32), 0.1, 1.9),
        "short_taps": centred(streams_of[4], (2, SHORT, D), SHORT ** -0.5, 2.0, ((2, 4),), jnp.float32),
        "medium_taps": centred(streams_of[5], (MEDIUM, D), MEDIUM ** -0.5, 0.5, ((1, 4),), jnp.float32),
        "pole_rates": draw_pole_rates(jax.random.fold_in(streams_of[9], 71), 0),
        "pole_residues": centred(streams_of[7], (MODES, D), MODES ** -0.5, 2.0, ((1, 4),), jnp.float32),
        "direct_term": centred(streams_of[8], (D,), 0.5, 3.0, ((0, 4),), jnp.float32),
    }


norm_eps = 1e-06

def depthwise(padded, flipped_taps):
    channels = padded.shape[1]
    result = lax.conv_general_dilated(padded[None], flipped_taps[:, None, :], window_strides=(1,), padding='VALID', dimension_numbers=('NWC', 'WIO', 'NWC'), feature_group_count=channels, precision=lax.Precision.HIGHEST)
    return result[0]

def causal_filter(gated, filter_taps):
    span = filter_taps.shape[0]
    padded = jnp.concatenate([jnp.zeros((span - 1, gated.shape[1]), jnp.float32), gated], axis=0)
    return depthwise(padded, jnp.flip(filter_taps, 0))

def modal_recurrence(gated, rates, residues, direct):
    decays = jnp.exp(-rates)
    weights = residues * jnp.sqrt(-jnp.expm1(-2.0 * rates))

    def advance(states, new_row):
        states = decays * states + new_row[None]
        return (states, lax.optimization_barrier(jnp.sum(weights * states, axis=0)))
    initial = jnp.zeros(rates.shape, jnp.float32)
    last_state, outputs = lax.scan(advance, initial, gated)
    return outputs + direct[None] * gated

def reference(inputs, query_fields, key_fields, norm_gain, short_taps, medium_taps, pole_rates, pole_residues, direct_term):
    values = inputs.astype(jnp.float32)
    inverse_rms = lax.rsqrt(lax.optimization_barrier(jnp.mean(values * values, axis=1)) + norm_eps)
    stream = (values * inverse_rms[:, None] * norm_gain[None]).astype(jnp.bfloat16)
    block_width = D // (N_CH * N_SEC)
    block_count = N_CH * N_SEC

    def one_block(block_index):
        offset = block_index * block_width

        def channel_cut(tables):
            return lax.dynamic_slice_in_dim(tables, offset, block_width, tables.ndim - 1)
        current = channel_cut(stream)
        for section in range(4):
            query_block = channel_cut(query_fields[section])
            key_block = channel_cut(key_fields[section])
            gated = key_block.astype(jnp.float32) * current.astype(jnp.float32)
            if section == 0:
                filtered = causal_filter(gated, channel_cut(short_taps[0]))
            elif section == 1:
                filtered = causal_filter(gated, channel_cut(medium_taps))
            elif section == 2:
                filtered = modal_recurrence(gated, channel_cut(pole_rates), channel_cut(pole_residues), channel_cut(direct_term))
            else:
                filtered = causal_filter(gated, channel_cut(short_taps[1]))
            current = (current.astype(jnp.float32) + query_block.astype(jnp.float32) * filtered).astype(jnp.bfloat16)
        return current
    blocks = lax.map(one_block, jnp.arange(block_count, dtype=jnp.int32))
    return jnp.transpose(blocks, (1, 0, 2)).reshape(TOKENS, D)
```

```python
import functools

import jax
import jax.numpy as jnp
from jax import lax
from jax.experimental import pallas as pl
from jax.experimental.pallas import tpu as pltpu
from jax.sharding import PartitionSpec as P

norm_eps = 1e-06
MESH = pl.DeviceIdType.MESH
LANES = 128
ROWS = 8
F32 = jnp.float32


def row_ids(shape):
    return lax.broadcasted_iota(jnp.int32, shape, 0)


def shifted(values, steps):
    if steps == 0:
        return values, jnp.zeros((ROWS, values.shape[1]), F32)
    moved = pltpu.roll(values, steps, 0)
    top = moved[:ROWS]
    inside = row_ids(top.shape) >= steps
    first = jnp.where(inside, top, 0.0)
    if values.shape[0] > ROWS:
        first = jnp.concatenate([first, moved[ROWS:]], axis=0)
    return first, jnp.where(inside, 0.0, top)


def filter_within(values, taps):
    length = values.shape[0]
    span = taps.shape[0]
    total = jnp.zeros(values.shape, F32)
    for step in range(min(ROWS, span)):
        moved, _ = shifted(values, step)
        for tap in range(step, min(span, length), ROWS):
            base = tap - step
            part = moved[: length - base] * taps[tap : tap + 1]
            if base:
                total = jnp.concatenate([total[:base], total[base:] + part], axis=0)
            else:
                total = total + part
    return total


def filter_before(history, taps, length):
    span = taps.shape[0]
    known = history.shape[0]
    total = jnp.zeros((length, history.shape[1]), F32)
    for step in range(min(ROWS, span)):
        moved, fallen = shifted(history, step)
        joined = jnp.concatenate([moved, fallen], axis=0)
        for tap in range(step, span, ROWS):
            base = tap - step
            reach = min(base + ROWS, length)
            part = joined[known - base : known - base + reach] * taps[tap : tap + 1]
            if reach < length:
                total = jnp.concatenate([total[:reach] + part, total[reach:]], axis=0)
            else:
                total = total + part
    return total


def kernel(
    sections,
    n_ctx,
    n_ch,
    inputs,
    query,
    key,
    gain,
    short,
    medium,
    rates,
    residues,
    direct,
    out,
    x_ref,
    gain_ref,
    short_ref,
    medium_ref,
    rate_ref,
    residue_ref,
    direct_ref,
    key_ref,
    query_ref,
    sums_sec,
    sums_ch,
    gated_ref,
    filtered_ref,
    stream_ref,
    tail_ref,
    rows_ref,
    state_ref,
    leaving_ref,
    taps_ref,
    age_ref,
    carry_ref,
    load_sem,
    key_send,
    key_recv,
    query_send,
    query_recv,
    sec_send,
    sec_recv,
    ch_send,
    ch_recv,
    ctx_send,
    ctx_recv,
):
    length, width = x_ref.shape
    modes = rate_ref.shape[0]
    sec = lax.axis_index("sec")
    ctx = lax.axis_index("ctx")
    ch = lax.axis_index("ch")
    has_before = ctx > 0
    has_after = ctx < n_ctx - 1

    def cut(index):
        return pl.ds(pl.multiple_of(index * width, width), width)

    mine = cut(sec)
    loads = [
        pltpu.make_async_copy(inputs, x_ref, load_sem.at[0]),
        pltpu.make_async_copy(rates.at[:, mine], rate_ref, load_sem.at[1]),
        pltpu.make_async_copy(residues.at[:, mine], residue_ref, load_sem.at[2]),
        pltpu.make_async_copy(direct.at[:, mine], direct_ref, load_sem.at[3]),
        pltpu.make_async_copy(gain.at[:, mine], gain_ref, load_sem.at[4]),
        pltpu.make_async_copy(short.at[:, :, mine], short_ref, load_sem.at[5]),
        pltpu.make_async_copy(medium.at[:, mine], medium_ref, load_sem.at[6]),
        pltpu.make_async_copy(key.at[0, :, mine], key_ref.at[sec], key_recv.at[sec]),
        pltpu.make_async_copy(query.at[0, :, mine], query_ref.at[sec], query_recv.at[sec]),
    ]
    for load in loads:
        load.start()

    sec_peers = [lax.rem(sec + step, sections) for step in range(1, sections)]
    ch_peers = [lax.rem(ch + step, n_ch) for step in range(1, n_ch)]
    barrier = pltpu.get_barrier_semaphore()
    for peer in sec_peers:
        pl.semaphore_signal(barrier, inc=1, device_id={"sec": peer}, device_id_type=MESH)
    for peer in ch_peers:
        pl.semaphore_signal(barrier, inc=1, device_id={"ch": peer}, device_id_type=MESH)

    @pl.when(has_before)
    def _():
        pl.semaphore_signal(barrier, inc=1, device_id={"ctx": ctx - 1}, device_id_type=MESH)

    @pl.when(has_after)
    def _():
        pl.semaphore_signal(barrier, inc=1, device_id={"ctx": ctx + 1}, device_id_type=MESH)

    loads[0].wait()
    squares = jnp.square(x_ref[...].astype(F32))
    folded = sum(squares[:, low : low + LANES] for low in range(0, width, LANES))
    partial = jnp.sum(folded.T, axis=0, keepdims=True)
    sums_sec[sec] = jnp.broadcast_to(partial, sums_sec.shape[1:])

    around = has_before.astype(jnp.int32) + has_after.astype(jnp.int32)
    pl.semaphore_wait(barrier, len(sec_peers) + len(ch_peers) + around)

    def remote(src, dst, send_sem, recv_sem, device):
        return pltpu.make_async_remote_copy(
            src_ref=src,
            dst_ref=dst,
            send_sem=send_sem,
            recv_sem=recv_sem,
            device_id=device,
            device_id_type=MESH,
        )

    sends = []
    for step, peer in enumerate(sec_peers):
        slot = sums_sec.at[sec]
        sends.append(remote(slot, slot, sec_send.at[step], sec_recv.at[sec], {"sec": peer}))
    for field, held, send_sem, recv_sem in (
        (key, key_ref, key_send, key_recv),
        (query, query_ref, query_send, query_recv),
    ):
        for step, peer in enumerate(sec_peers):
            sends.append(
                remote(
                    field.at[0, :, cut(peer)],
                    held.at[sec],
                    send_sem.at[step],
                    recv_sem.at[sec],
                    {"sec": peer},
                )
            )
    for send in sends:
        send.start()

    def arrived(ref, sem):
        pltpu.make_async_copy(ref, ref, sem).wait()

    for load in loads[1:4]:
        load.wait()
    offsets = row_ids((length, width)).astype(F32)
    rate_table = rate_ref[...]
    weights = residue_ref[...] * jnp.sqrt(1.0 - jnp.exp(-2.0 * rate_table))
    taps = jnp.where(row_ids((length, width)) == 0, direct_ref[...], 0.0)
    for mode in range(modes):
        part = weights[mode : mode + 1] * jnp.exp(-rate_table[mode : mode + 1] * offsets)
        carry_ref[mode] = part
        taps = taps + part
    taps_ref[...] = taps

    for peer in sec_peers:
        arrived(sums_sec.at[peer], sec_recv.at[peer])
    total = sums_sec[0]
    for index in range(1, sections):
        total = total + sums_sec[index]
    sums_ch[ch] = total
    for step, peer in enumerate(ch_peers):
        slot = sums_ch.at[ch]
        send = remote(slot, slot, ch_send.at[step], ch_recv.at[ch], {"ch": peer})
        send.start()
        sends.append(send)

    @pl.when(has_after)
    def _():
        ages = (length - 1.0) - offsets
        for mode in range(modes):
            age_ref[mode] = jnp.exp(-rate_table[mode : mode + 1] * ages)

    for load in loads[4:7]:
        load.wait()

    for peer in ch_peers:
        arrived(sums_ch.at[peer], ch_recv.at[peer])
    total = sums_ch[0]
    for index in range(1, n_ch):
        total = total + sums_ch[index]
    inverse = lax.rsqrt(total / (width * sections * n_ch) + norm_eps)
    scale = jnp.broadcast_to(inverse[:1], (length, length)).T[:, :1]
    stream = x_ref[...].astype(F32) * scale * gain_ref[...]
    stream_ref[...] = stream.astype(jnp.bfloat16).astype(F32)

    halves = [slice(low, low + LANES) for low in range(0, width, LANES)]
    after = {"ctx": lax.rem(ctx + 1, n_ctx)}

    def short_section(section, tap_set, tail_slot):
        hand = remote(
            gated_ref.at[section, pl.ds(length - ROWS, ROWS)],
            tail_ref.at[tail_slot],
            ctx_send.at[section],
            ctx_recv.at[section],
            after,
        )

        @pl.when(has_after)
        def _():
            hand.start()

        for half in halves:
            filtered_ref[:, half] = filter_within(
                gated_ref[section, :, half], short_ref[tap_set, :, half]
            )

        @pl.when(has_before)
        def _():
            hand.wait_recv()
            for half in halves:
                filtered_ref[:ROWS, half] += filter_before(
                    tail_ref[tail_slot, :, half], short_ref[tap_set, :, half], ROWS
                )

        return hand

    def medium_section(section):
        hand = remote(
            gated_ref.at[section], rows_ref, ctx_send.at[section], ctx_recv.at[section], after
        )

        @pl.when(has_after)
        def _():
            hand.start()

        for half in halves:
            filtered_ref[:, half] = filter_within(
                gated_ref[section, :, half], medium_ref[:, half]
            )

        @pl.when(has_before)
        def _():
            hand.wait_recv()
            for half in halves:
                filtered_ref[:, half] += filter_before(
                    rows_ref[:, half], medium_ref[:, half], length
                )

        return hand

    def long_section(section):
        hand = remote(leaving_ref, state_ref, ctx_send.at[section], ctx_recv.at[section], after)

        @pl.when(has_after)
        def _():
            for mode in range(modes):
                leaving_ref[mode : mode + 1] = jnp.sum(
                    age_ref[mode] * gated_ref[section], axis=0, keepdims=True
                )

        @pl.when(jnp.logical_and(has_after, jnp.logical_not(has_before)))
        def _():
            hand.start()

        @pl.when(has_before)
        def _():
            hand.wait_recv()

        @pl.when(jnp.logical_and(has_after, has_before))
        def _():
            leaving_ref[...] += jnp.exp(-length * rate_ref[...]) * state_ref[...]
            hand.start()

        for half in halves:
            filtered_ref[:, half] = filter_within(gated_ref[section, :, half], taps_ref[:, half])

        @pl.when(has_before)
        def _():
            entering = jnp.exp(-rate_ref[...]) * state_ref[...]
            for half in halves:
                carried = filtered_ref[:, half]
                for mode in range(modes):
                    carried = carried + carry_ref[mode, :, half] * entering[mode : mode + 1, half]
                filtered_ref[:, half] = carried

        return hand

    hands = []
    for section in range(sections):
        arrived(key_ref.at[section], key_recv.at[section])
        gated_ref[section] = key_ref[section].astype(F32) * stream_ref[...]
        if section == 1:
            hands.append(medium_section(section))
        elif section == 2:
            hands.append(long_section(section))
        else:
            hands.append(short_section(section, min(section, 1), min(section, 1)))
        arrived(query_ref.at[section], query_recv.at[section])
        stream = stream_ref[...] + query_ref[section].astype(F32) * filtered_ref[...]
        if section == sections - 1:
            out[...] = stream.astype(jnp.bfloat16)
        else:
            stream_ref[...] = stream.astype(jnp.bfloat16).astype(F32)

    for send in sends:
        send.wait_send()

    @pl.when(has_after)
    def _():
        for hand in hands:
            hand.wait_send()


def shards(
    inputs,
    query_fields,
    key_fields,
    norm_gain,
    short_taps,
    medium_taps,
    pole_rates,
    pole_residues,
    direct_term,
):
    sections = lax.axis_size("sec")
    n_ctx = lax.axis_size("ctx")
    n_ch = lax.axis_size("ch")
    length, width = inputs.shape
    modes = pole_rates.shape[0]
    shorts, short_span = short_taps.shape[:2]
    anywhere = pl.BlockSpec(memory_space=pl.ANY)
    dma = pltpu.SemaphoreType.DMA
    return pl.pallas_call(
        functools.partial(kernel, sections, n_ctx, n_ch),
        out_shape=jax.ShapeDtypeStruct((length, width), inputs.dtype),
        in_specs=[anywhere] * 9,
        out_specs=pl.BlockSpec(memory_space=pltpu.VMEM),
        scratch_shapes=[
            pltpu.VMEM((length, width), inputs.dtype),
            pltpu.VMEM((1, width), F32),
            pltpu.VMEM((shorts, short_span, width), F32),
            pltpu.VMEM((medium_taps.shape[0], width), F32),
            pltpu.VMEM((modes, width), F32),
            pltpu.VMEM((modes, width), F32),
            pltpu.VMEM((1, width), F32),
            pltpu.VMEM((sections, length, width), key_fields.dtype),
            pltpu.VMEM((sections, length, width), query_fields.dtype),
            pltpu.VMEM((sections, ROWS, length), F32),
            pltpu.VMEM((n_ch, ROWS, length), F32),
            pltpu.VMEM((sections, length, width), F32),
            pltpu.VMEM((length, width), F32),
            pltpu.VMEM((length, width), F32),
            pltpu.VMEM((2, ROWS, width), F32),
            pltpu.VMEM((length, width), F32),
            pltpu.VMEM((modes, width), F32),
            pltpu.VMEM((modes, width), F32),
            pltpu.VMEM((length, width), F32),
            pltpu.VMEM((modes, length, width), F32),
            pltpu.VMEM((modes, length, width), F32),
            dma((7,)),
            dma((sections - 1,)),
            dma((sections,)),
            dma((sections - 1,)),
            dma((sections,)),
            dma((sections - 1,)),
            dma((sections,)),
            dma((n_ch - 1,)),
            dma((n_ch,)),
            dma((sections,)),
            dma((sections,)),
        ],
        compiler_params=pltpu.CompilerParams(collective_id=0, has_side_effects=True),
    )(
        inputs,
        query_fields,
        key_fields,
        norm_gain[None],
        short_taps,
        medium_taps,
        pole_rates,
        pole_residues,
        direct_term[None],
    )


def solution(mesh):
    in_specs = (
        P("ctx", ("ch", "sec")),
        P("sec", "ctx", "ch"),
        P("sec", "ctx", "ch"),
        P("ch"),
        P(None, None, "ch"),
        P(None, "ch"),
        P(None, "ch"),
        P(None, "ch"),
        P("ch"),
    )
    out_specs = P("ctx", ("ch", "sec"))
    return jax.shard_map(shards, mesh=mesh, in_specs=in_specs, out_specs=out_specs, check_vma=False)
```

```python
import functools

import jax
import jax.numpy as jnp
from jax import lax
from jax.experimental import pallas as pl
from jax.experimental.pallas import tpu as pltpu
from jax.sharding import PartitionSpec as P

norm_eps = 1e-06
MESH = pl.DeviceIdType.MESH
LANES = 128
ROWS = 8
F32 = jnp.float32


def row_ids(shape):
    return lax.broadcasted_iota(jnp.int32, shape, 0)


def shifted(values, steps):
    if steps == 0:
        return values, jnp.zeros((ROWS, values.shape[1]), F32)
    moved = pltpu.roll(values, steps, 0)
    top = moved[:ROWS]
    inside = row_ids(top.shape) >= steps
    first = jnp.where(inside, top, 0.0)
    if values.shape[0] > ROWS:
        first = jnp.concatenate([first, moved[ROWS:]], axis=0)
    return first, jnp.where(inside, 0.0, top)


def filter_within(values, taps):
    length = values.shape[0]
    span = taps.shape[0]
    total = jnp.zeros(values.shape, F32)
    for step in range(min(ROWS, span)):
        moved, _ = shifted(values, step)
        for tap in range(step, min(span, length), ROWS):
            base = tap - step
            part = moved[: length - base] * taps[tap : tap + 1]
            if base:
                total = jnp.concatenate([total[:base], total[base:] + part], axis=0)
            else:
                total = total + part
    return total


def filter_before(history, taps, length, own=0):
    span = taps.shape[0]
    known = history.shape[0] - own
    total = jnp.zeros((length, history.shape[1]), F32)
    for step in range(min(ROWS, span)):
        moved, fallen = shifted(history, step)
        joined = jnp.concatenate([moved, fallen], axis=0)
        for tap in range(step, span, ROWS):
            base = tap - step
            reach = min(base + ROWS + own, length)
            part = joined[known - base : known - base + reach] * taps[tap : tap + 1]
            if reach < length:
                total = jnp.concatenate([total[:reach] + part, total[reach:]], axis=0)
            else:
                total = total + part
    return total


def kernel(
    sections,
    n_ctx,
    n_ch,
    inputs,
    query,
    key,
    gain,
    short,
    medium,
    rates,
    residues,
    direct,
    out,
    x_ref,
    gain_ref,
    short_ref,
    medium_ref,
    rate_ref,
    residue_ref,
    direct_ref,
    key_ref,
    query_ref,
    sums_sec,
    sums_ch,
    gated_ref,
    filtered_ref,
    stream_ref,
    tail_ref,
    rows_ref,
    state_ref,
    leaving_ref,
    taps_ref,
    age_ref,
    carry_ref,
    top_ref,
    load_sem,
    key_send,
    key_recv,
    query_send,
    query_recv,
    sec_send,
    sec_recv,
    ch_send,
    ch_recv,
    ctx_send,
    ctx_recv,
):
    length, width = x_ref.shape
    modes = rate_ref.shape[0]
    sec = lax.axis_index("sec")
    ctx = lax.axis_index("ctx")
    ch = lax.axis_index("ch")
    has_before = ctx > 0
    has_after = ctx < n_ctx - 1

    def cut(index):
        return pl.ds(pl.multiple_of(index * width, width), width)

    mine = cut(sec)
    loads = [
        pltpu.make_async_copy(inputs, x_ref, load_sem.at[0]),
        pltpu.make_async_copy(rates.at[:, mine], rate_ref, load_sem.at[1]),
        pltpu.make_async_copy(residues.at[:, mine], residue_ref, load_sem.at[2]),
        pltpu.make_async_copy(direct.at[:, mine], direct_ref, load_sem.at[3]),
        pltpu.make_async_copy(gain.at[:, mine], gain_ref, load_sem.at[4]),
        pltpu.make_async_copy(short.at[:, :, mine], short_ref, load_sem.at[5]),
        pltpu.make_async_copy(medium.at[:, mine], medium_ref, load_sem.at[6]),
        pltpu.make_async_copy(key.at[0, :, mine], key_ref.at[sec], key_recv.at[sec]),
        pltpu.make_async_copy(query.at[0, :, mine], query_ref.at[sec], query_recv.at[sec]),
    ]
    for load in loads:
        load.start()

    sec_peers = [lax.rem(sec + step, sections) for step in range(1, sections)]
    ch_peers = [lax.rem(ch + step, n_ch) for step in range(1, n_ch)]
    barrier = pltpu.get_barrier_semaphore()
    for peer in sec_peers:
        pl.semaphore_signal(barrier, inc=1, device_id={"sec": peer}, device_id_type=MESH)
    for peer in ch_peers:
        pl.semaphore_signal(barrier, inc=1, device_id={"ch": peer}, device_id_type=MESH)

    @pl.when(has_before)
    def _():
        pl.semaphore_signal(barrier, inc=1, device_id={"ctx": ctx - 1}, device_id_type=MESH)

    @pl.when(has_after)
    def _():
        pl.semaphore_signal(barrier, inc=1, device_id={"ctx": ctx + 1}, device_id_type=MESH)

    loads[0].wait()
    squares = jnp.square(x_ref[...].astype(F32))
    folded = sum(squares[:, low : low + LANES] for low in range(0, width, LANES))
    partial = jnp.sum(folded.T, axis=0, keepdims=True)
    sums_sec[sec] = partial

    around = has_before.astype(jnp.int32) + has_after.astype(jnp.int32)
    pl.semaphore_wait(barrier, len(sec_peers) + len(ch_peers) + around)

    def remote(src, dst, send_sem, recv_sem, device):
        return pltpu.make_async_remote_copy(
            src_ref=src,
            dst_ref=dst,
            send_sem=send_sem,
            recv_sem=recv_sem,
            device_id=device,
            device_id_type=MESH,
        )

    sends = []
    for step, peer in enumerate(sec_peers):
        slot = sums_sec.at[sec]
        sends.append(remote(slot, slot, sec_send.at[step], sec_recv.at[sec], {"sec": peer}))
    for field, held, send_sem, recv_sem in (
        (key, key_ref, key_send, key_recv),
        (query, query_ref, query_send, query_recv),
    ):
        for step, peer in enumerate(sec_peers):
            sends.append(
                remote(
                    field.at[0, :, cut(peer)],
                    held.at[sec],
                    send_sem.at[step],
                    recv_sem.at[sec],
                    {"sec": peer},
                )
            )
    for send in sends:
        send.start()

    def arrived(ref, sem):
        pltpu.make_async_copy(ref, ref, sem).wait()

    for load in loads[1:4]:
        load.wait()
    offsets = row_ids((length, width)).astype(F32)
    rate_table = rate_ref[...]
    weights = residue_ref[...] * jnp.sqrt(1.0 - jnp.exp(-2.0 * rate_table))
    taps = jnp.where(row_ids((length, width)) == 0, direct_ref[...], 0.0)
    for mode in range(modes):
        part = weights[mode : mode + 1] * jnp.exp(-rate_table[mode : mode + 1] * offsets)
        carry_ref[mode] = part
        taps = taps + part
    taps_ref[...] = taps

    for peer in sec_peers:
        arrived(sums_sec.at[peer], sec_recv.at[peer])
    total = sums_sec[0]
    for index in range(1, sections):
        total = total + sums_sec[index]
    sums_ch[ch] = total
    for step, peer in enumerate(ch_peers):
        slot = sums_ch.at[ch]
        send = remote(slot, slot, ch_send.at[step], ch_recv.at[ch], {"ch": peer})
        send.start()
        sends.append(send)

    @pl.when(has_after)
    def _():
        ages = (length - 1.0) - offsets
        for mode in range(modes):
            age_ref[mode] = jnp.exp(-rate_table[mode : mode + 1] * ages)

    for load in loads[4:7]:
        load.wait()

    for peer in ch_peers:
        arrived(sums_ch.at[peer], ch_recv.at[peer])
    total = sums_ch[0]
    for index in range(1, n_ch):
        total = total + sums_ch[index]
    inverse = lax.rsqrt(total / (width * sections * n_ch) + norm_eps)
    scale = jnp.broadcast_to(inverse[:1], (length, length)).T[:, :1]
    stream = x_ref[...].astype(F32) * scale * gain_ref[...]
    stream_ref[...] = stream.astype(jnp.bfloat16).astype(F32)

    halves = [slice(low, low + LANES) for low in range(0, width, LANES)]
    after = {"ctx": lax.rem(ctx + 1, n_ctx)}

    def short_section(section, tap_set, tail_slot):
        hand = remote(
            gated_ref.at[section, pl.ds(length - ROWS, ROWS)],
            tail_ref.at[tail_slot],
            ctx_send.at[section],
            ctx_recv.at[section],
            after,
        )

        @pl.when(has_after)
        def _():
            hand.start()

        for half in halves:
            filtered_ref[:, half] = filter_within(
                gated_ref[section, :, half], short_ref[:, tap_set, half]
            )

        if section:

            @pl.when(has_before)
            def _():
                hand.wait_recv()
                finish_top(tail_slot, tap_set)

        return hand

    def finish_top(tail_slot, tap_set):
        for half in halves:
            filtered_ref[:ROWS, half] += filter_before(
                tail_ref[tail_slot, :, half], short_ref[:, tap_set, half], ROWS
            )

    def medium_section(section, earlier):
        @pl.when(has_before)
        def _():
            gated_ref[section, :ROWS] = jnp.zeros((ROWS, width), F32)

        hand = remote(
            gated_ref.at[section], rows_ref, ctx_send.at[section], ctx_recv.at[section], after
        )

        @pl.when(jnp.logical_and(has_after, jnp.logical_not(has_before)))
        def _():
            hand.start()

        for half in halves:
            filtered_ref[:, half] = filter_within(
                gated_ref[section, :, half], medium_ref[:, half]
            )

        @pl.when(has_before)
        def _():
            earlier.wait_recv()
            for half in halves:
                added = filter_before(tail_ref[0, :, half], short_ref[:, 0, half], ROWS)
                gate = query_ref[section - 1, :ROWS, half].astype(F32)
                top = top_ref[0, :, half] + gate * (top_ref[1, :, half] + added)
                top = top.astype(jnp.bfloat16).astype(F32)
                stream_ref[:ROWS, half] = top
                gated_ref[section, :ROWS, half] = key_ref[section, :ROWS, half].astype(F32) * top

        @pl.when(jnp.logical_and(has_after, has_before))
        def _():
            hand.start()

        @pl.when(has_before)
        def _():
            hand.wait_recv()
            for half in halves:
                history = jnp.concatenate(
                    [rows_ref[:, half], gated_ref[section, :ROWS, half]], axis=0
                )
                filtered_ref[:, half] += filter_before(
                    history, medium_ref[:, half], length, ROWS
                )

        return hand

    def long_section(section):
        hand = remote(leaving_ref, state_ref, ctx_send.at[section], ctx_recv.at[section], after)

        @pl.when(has_after)
        def _():
            for mode in range(modes):
                leaving_ref[mode : mode + 1] = jnp.sum(
                    age_ref[mode] * gated_ref[section], axis=0, keepdims=True
                )

        @pl.when(jnp.logical_and(has_after, jnp.logical_not(has_before)))
        def _():
            hand.start()

        @pl.when(has_before)
        def _():
            hand.wait_recv()

        @pl.when(jnp.logical_and(has_after, has_before))
        def _():
            leaving_ref[...] += jnp.exp(-length * rate_ref[...]) * state_ref[...]
            hand.start()

        for half in halves:
            filtered_ref[:, half] = filter_within(gated_ref[section, :, half], taps_ref[:, half])

        @pl.when(has_before)
        def _():
            entering = jnp.exp(-rate_ref[...]) * state_ref[...]
            for half in halves:
                carried = filtered_ref[:, half]
                for mode in range(modes):
                    carried = carried + carry_ref[mode, :, half] * entering[mode : mode + 1, half]
                filtered_ref[:, half] = carried

        return hand

    hands = []
    for section in range(sections):
        arrived(key_ref.at[section], key_recv.at[section])
        gated_ref[section] = key_ref[section].astype(F32) * stream_ref[...]
        if section == 1:
            hands.append(medium_section(section, hands[0]))
        elif section == 2:
            hands.append(long_section(section))
        else:
            hands.append(short_section(section, min(section, 1), min(section, 1)))
        arrived(query_ref.at[section], query_recv.at[section])
        if section == 0:
            top_ref[0] = stream_ref[:ROWS]
            top_ref[1] = filtered_ref[:ROWS]
        stream = stream_ref[...] + query_ref[section].astype(F32) * filtered_ref[...]
        if section == sections - 1:
            out[...] = stream.astype(jnp.bfloat16)
        else:
            stream_ref[...] = stream.astype(jnp.bfloat16).astype(F32)

    for send in sends:
        send.wait_send()

    @pl.when(has_after)
    def _():
        for hand in hands:
            hand.wait_send()


def shards(
    inputs,
    query_fields,
    key_fields,
    norm_gain,
    short_taps,
    medium_taps,
    pole_rates,
    pole_residues,
    direct_term,
):
    sections = lax.axis_size("sec")
    n_ctx = lax.axis_size("ctx")
    n_ch = lax.axis_size("ch")
    length, width = inputs.shape
    modes = pole_rates.shape[0]
    shorts, short_span = short_taps.shape[:2]
    hbm = pl.BlockSpec(memory_space=pltpu.HBM)
    anywhere = pl.BlockSpec(memory_space=pl.ANY)
    dma = pltpu.SemaphoreType.DMA
    return pl.pallas_call(
        functools.partial(kernel, sections, n_ctx, n_ch),
        out_shape=jax.ShapeDtypeStruct((length, width), inputs.dtype),
        in_specs=[anywhere] * 9,
        out_specs=pl.BlockSpec(memory_space=pltpu.VMEM),
        scratch_shapes=[
            pltpu.VMEM((length, width), inputs.dtype),
            pltpu.VMEM((1, width), F32),
            pltpu.VMEM((short_span, shorts, width), F32),
            pltpu.VMEM((medium_taps.shape[0], width), F32),
            pltpu.VMEM((modes, width), F32),
            pltpu.VMEM((modes, width), F32),
            pltpu.VMEM((1, width), F32),
            pltpu.VMEM((sections, length, width), key_fields.dtype),
            pltpu.VMEM((sections, length, width), query_fields.dtype),
            pltpu.VMEM((sections, 1, length), F32),
            pltpu.VMEM((n_ch, 1, length), F32),
            pltpu.VMEM((sections, length, width), F32),
            pltpu.VMEM((length, width), F32),
            pltpu.VMEM((length, width), F32),
            pltpu.VMEM((2, ROWS, width), F32),
            pltpu.VMEM((length, width), F32),
            pltpu.VMEM((modes, width), F32),
            pltpu.VMEM((modes, width), F32),
            pltpu.VMEM((length, width), F32),
            pltpu.VMEM((modes, length, width), F32),
            pltpu.VMEM((modes, length, width), F32),
            pltpu.VMEM((2, ROWS, width), F32),
            dma((7,)),
            dma((sections - 1,)),
            dma((sections,)),
            dma((sections - 1,)),
            dma((sections,)),
            dma((sections - 1,)),
            dma((sections,)),
            dma((n_ch - 1,)),
            dma((n_ch,)),
            dma((sections,)),
            dma((sections,)),
        ],
        compiler_params=pltpu.CompilerParams(collective_id=0, has_side_effects=True),
    )(
        inputs,
        query_fields,
        key_fields,
        norm_gain[None],
        jnp.swapaxes(short_taps, 0, 1),
        medium_taps,
        pole_rates,
        pole_residues,
        direct_term[None],
    )


def solution(mesh):
    in_specs = (
        P("ctx", ("ch", "sec")),
        P("sec", "ctx", "ch"),
        P("sec", "ctx", "ch"),
        P("ch"),
        P(None, None, "ch"),
        P(None, "ch"),
        P(None, "ch"),
        P(None, "ch"),
        P("ch"),
    )
    out_specs = P("ctx", ("ch", "sec"))
    return jax.shard_map(shards, mesh=mesh, in_specs=in_specs, out_specs=out_specs, check_vma=False)
```
